32 devices in a mesh: tile: 8 (over z, x), depth: 4 (over y, core).
Axes of the slice: x: 2, y: 2, z: 4, core: 2. Of those that a mesh axis runs over, the one named last changes fastest.
Arguments:
- density: float32 [64, 128, 128], P('depth', 'tile'), may hold values from 0.5 to 2
- momentum: float32 [3, 64, 128, 128], P(None, 'depth', 'tile'), may hold values from -4 to 4
- magnetic: float32 [3, 64, 128, 128], P(None, 'depth', 'tile'), may hold values from -4 to 4
- energy: float32 [64, 128, 128], P('depth', 'tile'), may hold values from 2 to 4
- shifts: int32 [24], replicated, may hold values from 0 to 55, as said below
- levels: int32 [24], replicated, may hold values from 0 to 63, as said below
Outputs:
- new_state: float32 [8, 64, 128, 128], P(None, 'depth', 'tile')
- intensity: float32 [48, 128, 128], P(None, 'tile', 'depth')
The draws below stay inside these ranges and needn't reach their ends.
Inputs may be any that keep to these rules, and one draw needn't show every extreme that they name: shifts[k] = (1732 (levels[k] - levels[0]) + 1000) // 2000, the nearest whole column to tan(60 degrees) times the depth gap at half a column per level; the last is exactly 55. 24 distinct levels in ascending order, the first 0 and the last 63; each depth slab of 16 consecutive levels holds at most 8 of them, and some slab exactly 8.
All inputs are finite; a program needn't handle non-finite values.
Results may differ from the reference program's by a relative error of at most 0.000054.
Values sent between devices are 32-bit elements; how exact they have to be, the bound alone decides.
A program may use at most 64 MiB of HBM per device.

```python
import math
import jax
import jax.numpy as jnp
from jax import lax

CZ = 16
NY = 128
MOST = 8
W = 48
LEVELS = 64
X = 128
SYN = 24
N_DEPTH = 4


def pick_levels(key):
    total = CZ * N_DEPTH
    first_key, slab_key, second_key = jax.random.split(jax.random.fold_in(key, 7), 3)
    index = jnp.arange(total, dtype=jnp.int32)
    slab = index // CZ
    ends = (index == 0) | (index == total - 1)
    first = jax.random.permutation(first_key, total).astype(jnp.int32)
    first = jnp.where(ends, -1, first).astype(jnp.int32)
    same = slab[:, None] == slab[None, :]
    rank = jnp.sum(same & (first[None, :] < first[:, None]), axis=1)
    chosen = jax.random.randint(slab_key, (), 0, N_DEPTH)
    candidate = rank < MOST
    busy = slab == chosen
    others = candidate & jnp.logical_not(busy)
    second = jax.random.permutation(second_key, total).astype(jnp.int32)
    second = jnp.where(ends, -1, second).astype(jnp.int32)
    other_rank = jnp.sum(others[None, :] & (second[None, :] < second[:, None]), axis=1)
    picked = candidate & busy | others & (other_rank < SYN - MOST)
    return jnp.nonzero(picked, size=SYN)[0].astype(jnp.int32)


def draw_levels(key, part):
    return pick_levels(key)


def draw_shifts(key, part):
    chosen_levels = pick_levels(key)
    gap = chosen_levels - chosen_levels[0]
    return ((1732 * gap + 1000) // 2000).astype(jnp.int32)


def steps_of(own_key, shape, cuts, low, high):
    def one(dim, shards_of):
        draws = jax.random.uniform(jax.random.fold_in(jax.random.fold_in(own_key, 6), dim), (shards_of,), jnp.float32, low / len(cuts), high / len(cuts))
        return jnp.repeat(jnp.exp(draws), shape[dim] // shards_of).reshape((-1,) + (1,) * (len(shape) - dim - 1))

    level = one(*cuts[0])
    for cut in cuts[1:]:
        level = level * one(*cut)
    return level


def bell_draw(key, shape, spread, reach, cuts=(), kind=jnp.bfloat16):
    gain = steps_of(key, shape, cuts, -0.22, 0.18) if cuts else 1.0
    drawn = jax.random.normal(key, shape, jnp.float32) * spread * gain
    return jnp.minimum(jnp.maximum(drawn, -reach), reach).astype(kind)


def setup_inputs(seed: int = 0) -> dict:
    seeds = jax.random.split(jax.random.key(seed), 7)
    return {
        "density": jnp.clip(jnp.exp(math.log(2.0) - 1.3862944 * jax.random.uniform(seeds[0], (LEVELS, X, NY), jnp.float32) ** steps_of(seeds[0], (LEVELS, X, NY), ((0, 4), (1, 8)), -0.2, 0.2)), 0.5, 2.0),
        "momentum": bell_draw(seeds[1], (3, LEVELS, X, NY), 0.5, 4.0, ((1, 4), (2, 8)), jnp.float32),
        "magnetic": bell_draw(seeds[2], (3, LEVELS, X, NY), 0.5, 4.0, ((1, 4), (2, 8)), jnp.float32),
        "energy": jnp.clip(2.0 + 2.0 * jax.random.uniform(seeds[3], (LEVELS, X, NY), jnp.float32) ** steps_of(seeds[3], (LEVELS, X, NY), ((0, 4), (1, 8)), -0.2, 0.2), 2.0, 4.0),
        "shifts": draw_shifts(jax.random.fold_in(seeds[6], 71), 0),
        "levels": draw_levels(jax.random.fold_in(seeds[6], 71), 0),
    }


GAMMA = 5.0 / 3.0
SECTION = 0.02
GRAVITY = 0.5
SIN_VIEW = 0.8660254037844386
COS_VIEW = 0.5
STRENGTH = 4.0
SPACING = 0.25


def derive(padded, axis, count):
    def layer(offset):
        return lax.slice_in_dim(padded, offset, offset + count, axis=axis)
    return (45.0 * (layer(4) - layer(2)) - 9.0 * (layer(5) - layer(1)) + (layer(6) - layer(0))) / 60.0


def flux(state, comp):
    rho = state[0]
    moment = state[1:4]
    field = state[4:7]
    energy = state[7]
    velocity = moment / rho
    field_sq = jnp.sum(field * field, axis=0)
    pressure = (GAMMA - 1.0) * (energy - 0.5 * jnp.sum(moment * velocity, axis=0) - 0.5 * field_sq)
    total = pressure + 0.5 * field_sq
    along = velocity[comp]
    normal = field[comp]
    flux_mom = (moment * along - field * normal).at[comp].add(total)
    flux_mag = along * field - normal * velocity
    flux_energy = (energy + total) * along - normal * jnp.sum(velocity * field, axis=0)
    return jnp.concatenate([moment[comp][None], flux_mom, flux_mag, flux_energy[None]], axis=0)


def tendency(along_x, along_y, along_z, state):
    depth_cells, width_cells, cross_cells = state.shape[1], state.shape[2], state.shape[3]
    rate = -(derive(flux(along_x, 0), 2, width_cells) + derive(flux(along_y, 1), 3, cross_cells) + derive(flux(along_z, 2), 1, depth_cells))
    rate = rate.at[3].add(GRAVITY * state[0])
    rate = rate.at[7].add(GRAVITY * state[3])
    return rate


def line_fields(new_state):
    dens = 0.5 + jax.nn.softplus(new_state[0])
    speed = (COS_VIEW * new_state[3] + SIN_VIEW * new_state[1]) / dens
    field_sq = jnp.sum(new_state[4:7] * new_state[4:7], axis=0)
    source = jax.nn.softplus(new_state[7] - 0.5 * field_sq) / dens
    return jnp.stack([dens, speed, source], axis=1)


def reference(density, momentum, magnetic, energy, shifts, levels):
    state = jnp.concatenate([density[None], momentum, magnetic, energy[None]], axis=0)
    along_x = jnp.pad(state, ((0, 0), (0, 0), (3, 3), (0, 0)), mode="wrap")
    along_y = jnp.pad(state, ((0, 0), (0, 0), (0, 0), (3, 3)), mode="wrap")
    along_z = jnp.pad(state, ((0, 0), (3, 3), (0, 0), (0, 0)), mode="edge")
    new_state = state + SECTION * tendency(along_x, along_y, along_z, state)
    fields = line_fields(new_state)[levels]
    count = levels.shape[0]
    width_cells = fields.shape[2]
    index = (jnp.arange(width_cells, dtype=jnp.int32)[None, :] + shifts[:, None]) % width_cells
    index = jnp.broadcast_to(index[:, None, :, None], fields.shape).astype(jnp.int32)
    sheared = jnp.take_along_axis(fields, index, axis=2)
    dens = sheared[:, 0]
    speed = sheared[:, 1]
    source = sheared[:, 2]

    def emergent(wave):
        offset = (wave.astype(jnp.float32) - 0.5 * (W - 1)) * SPACING
        gap = offset - speed
        dtau = (2.0 / count) * dens * (1.0 + STRENGTH * jnp.exp(-gap * gap))
        running = jnp.cumsum(dtau, axis=0)
        above = jnp.concatenate([jnp.zeros_like(dtau[:1]), running[:-1]], axis=0)
        inner = jnp.sum(source * jnp.exp(-above) * (1.0 - jnp.exp(-dtau)), axis=0)
        return inner + source[count - 1] * jnp.exp(-running[count - 1])

    intensity = lax.map(emergent, jnp.arange(W, dtype=jnp.int32))
    return new_state, intensity
```

```python
import jax
import jax.numpy as jnp
from jax import lax
from jax.sharding import PartitionSpec as P

W = 48
MOST = 8


GAMMA = 5.0 / 3.0
SECTION = 0.02
GRAVITY = 0.5
SIN_VIEW = 0.8660254037844386
COS_VIEW = 0.5
STRENGTH = 4.0
SPACING = 0.25


def shifted(block, axis, distance):
    devices = range(lax.axis_size(axis))
    route = [((i - distance) % len(devices), i) for i in devices]
    return lax.ppermute(block, axis, route)


def padded_2(cells, sides, width, closed):
    for axis, dim in sides:
        count = lax.axis_size(axis)
        ends = count if closed else count - 1
        head = lax.slice_in_dim(cells, 0, width, axis=dim)
        tail = lax.slice_in_dim(cells, cells.shape[dim] - width, cells.shape[dim], axis=dim)
        cells = jnp.concatenate(
            [
                lax.ppermute(tail, axis, [(i, (i + 1) % count) for i in range(ends)]),
                cells,
                lax.ppermute(head, axis, [((i + 1) % count, i) for i in range(ends)]),
            ],
            axis=dim,
        )
    return cells


def derive(padded, axis, count):

    def layer(offset):
        return lax.slice_in_dim(padded, offset, offset + count, axis=axis)

    return (
        45.0 * (layer(4) - layer(2)) - 9.0 * (layer(5) - layer(1)) + (layer(6) - layer(0))
    ) / 60.0


def flux(state, comp):
    rho = state[0]
    moment = state[1:4]
    field = state[4:7]
    energy = state[7]
    velocity = moment / rho
    field_sq = jnp.sum(field * field, axis=0)
    pressure = (GAMMA - 1.0) * (energy - 0.5 * jnp.sum(moment * velocity, axis=0) - 0.5 * field_sq)
    total = pressure + 0.5 * field_sq
    along = velocity[comp]
    normal = field[comp]
    flux_mom = (moment * along - field * normal).at[comp].add(total)
    flux_mag = along * field - normal * velocity
    flux_energy = (energy + total) * along - normal * jnp.sum(velocity * field, axis=0)
    return jnp.concatenate([moment[comp][None], flux_mom, flux_mag, flux_energy[None]], axis=0)


def tendency(along_x, along_y, along_z, state):
    depth_cells, width_cells, cross_cells = (state.shape[1], state.shape[2], state.shape[3])
    rate = -(
        derive(flux(along_x, 0), 2, width_cells)
        + derive(flux(along_y, 1), 3, cross_cells)
        + derive(flux(along_z, 2), 1, depth_cells)
    )
    rate = rate.at[3].add(GRAVITY * state[0])
    rate = rate.at[7].add(GRAVITY * state[3])
    return rate


def line_fields(new_state):
    dens = 0.5 + jax.nn.softplus(new_state[0])
    speed = (COS_VIEW * new_state[3] + SIN_VIEW * new_state[1]) / dens
    field_sq = jnp.sum(new_state[4:7] * new_state[4:7], axis=0)
    source = jax.nn.softplus(new_state[7] - 0.5 * field_sq) / dens
    return jnp.stack([dens, speed, source], axis=1)


def column_shift(level):
    return (1732 * level + 1000) // 2000


def shear(rows, row_shift, depth_cells):
    cells = rows.shape[2]
    tiles = lax.axis_size("tile")
    slabs = lax.axis_size("depth")
    first = [column_shift(d * depth_cells) // cells for d in range(slabs)]
    last = [
        (column_shift((d + 1) * depth_cells - 1) + cells - 1) // cells for d in range(slabs)
    ]
    count = max(high - low + 1 for low, high in zip(first, last))
    pieces = []
    for turn in range(count):
        route = [
            (((t + first[d] + turn) % tiles) * slabs + d, t * slabs + d)
            for t in range(tiles)
            for d in range(slabs)
            if first[d] + turn <= last[d]
        ]
        pieces.append(lax.ppermute(rows, ("tile", "depth"), route))
    joined = jnp.concatenate(pieces, axis=2)
    lowest = lax.axis_index("depth") * depth_cells
    offset = row_shift - column_shift(lowest) // cells * cells
    target = jnp.arange(cells, dtype=jnp.int32)
    anchor = jnp.arange(count * cells, dtype=jnp.int32)
    select = (anchor[None, None, :] == target[None, :, None] + offset[:, None, None]).astype(
        jnp.float32
    )
    return jnp.einsum("lcxa,lwx->lcwa", joined, select, precision=lax.Precision.HIGHEST)


def regroup(rows):
    return lax.all_to_all(rows, "depth", split_axis=3, concat_axis=0, tiled=True)


def emergent(columns):
    positions = columns.shape[0]
    flat = columns.reshape(positions, 3, -1)
    dens = flat[:, 0]
    speed = flat[:, 1]
    source = flat[:, 2]
    waves = (jnp.arange(W, dtype=jnp.float32) - 0.5 * (W - 1)) * SPACING
    gap = waves[:, None, None] - speed[None]
    dtau = 2.0 / positions * dens[None] * (1.0 + STRENGTH * jnp.exp(-gap * gap))
    order = jnp.arange(positions, dtype=jnp.int32)
    earlier = (order[None, :] < order[:, None]).astype(jnp.float32)
    above = jnp.einsum("kj,wjc->wkc", earlier, dtau, precision=lax.Precision.HIGHEST)
    inner = jnp.sum(source[None] * jnp.exp(-above) * (1.0 - jnp.exp(-dtau)), axis=1)
    total = inner + source[-1][None] * jnp.exp(-above[:, -1] - dtau[:, -1])
    return total.reshape((W,) + columns.shape[2:])


def per_device(density, momentum, magnetic, energy, shifts, levels):
    state = jnp.concatenate([density[None], momentum, magnetic, energy[None]], axis=0)
    count_vars, depth_cells, width_cells, cross_cells = state.shape
    depth_at = lax.axis_index("depth")
    slabs = lax.axis_size("depth")
    along_x = padded_2(state, (("tile", 2),), 3, True)
    padded = padded_2(state, (("depth", 1),), 3, False)
    rim_shape = (count_vars, 3, width_cells, cross_cells)
    head = jnp.where(depth_at == 0, jnp.broadcast_to(state[:, :1], rim_shape), padded[:, :3])
    tail = jnp.where(
        depth_at == slabs - 1,
        jnp.broadcast_to(state[:, -1:], rim_shape),
        padded[:, depth_cells + 3 :],
    )
    along_z = jnp.concatenate([head, state, tail], axis=1)
    along_y = jnp.pad(state, ((0, 0), (0, 0), (0, 0), (3, 3)), mode="wrap")
    new_state = state + SECTION * tendency(along_x, along_y, along_z, state)
    fields = line_fields(new_state)
    most = min(MOST, depth_cells)
    lowest = depth_at * depth_cells
    ahead = jnp.sum((levels < lowest).astype(jnp.int32))
    position = jnp.minimum(ahead + jnp.arange(most, dtype=jnp.int32), levels.shape[0] - 1)
    held = jnp.clip(levels[position] - lowest, 0, depth_cells - 1)
    sheared = shear(fields[held], shifts[position], depth_cells)
    slab = levels // depth_cells
    before = jnp.sum((levels[None, :] < (slab * depth_cells)[:, None]).astype(jnp.int32), axis=1)
    rank = jnp.arange(levels.shape[0], dtype=jnp.int32) - before
    columns = regroup(sheared)[slab * most + rank]
    intensity = emergent(columns)
    return (new_state, intensity)


def solution(mesh):
    return jax.shard_map(
        per_device,
        mesh=mesh,
        in_specs=(
            P("depth", "tile", None),
            P(None, "depth", "tile", None),
            P(None, "depth", "tile", None),
            P("depth", "tile", None),
            P(),
            P(),
        ),
        out_specs=(P(None, "depth", "tile", None), P(None, "tile", "depth")),
        check_vma=False,
    )
```
